32 devices in a mesh: seq: 8 (over z, y), tensor: 4 (over x, core).
Axes of the slice: x: 2, y: 2, z: 4, core: 2. Of those that a mesh axis runs over, the one named last changes fastest.
Arguments:
- queries: bfloat16 [768, 4096], P('seq', 'tensor'), may hold values from -96 to 96
- keys: bfloat16 [768, 1024], P('seq', 'tensor'), may hold values from -96 to 96
- values: bfloat16 [768, 1024], P('seq', 'tensor'), may hold values from -6 to 6
- out_weight: bfloat16 [4096, 4096], P('tensor'), may hold values from -0.09375 to 0.09375
- doc_lengths: int32 [16], replicated, may hold values from 1 to 192, 768 in all
- stretch_place: int32 [16], replicated, may hold values from 0 to 15, each once
Outputs:
- output: bfloat16 [768, 4096], P('seq', 'tensor')
The draws below stay inside these ranges and needn't reach their ends.
Inputs may be any that keep to these rules, and one draw needn't show every extreme that they name: `stretch_place`: each stored block number appears once. `doc_lengths`: the lengths sum to 768; the longest is exactly 192.
All inputs are finite; a program needn't handle non-finite values.
Results may differ from the reference program's by a relative error of at most 0.015.
Values may be sent and summed in bfloat16 or wider, within the bound.
A program may use at most 64 MiB of HBM per device.

```python
import math
import jax
import jax.numpy as jnp
import numpy as np
from jax import lax

D = 4096
HEADS = 32
KV_HEADS = 8
HD = 128
TOK_DEV = 96
DOCS = 16
TOKENS = 768
BLOCKS = 16
DOC_MOST = 192


def draw_pair(key):
    base = jax.random.fold_in(key, 7)
    key_query, key_key = jax.random.split(base, 2)
    query_draw = jax.random.normal(key_query, (TOKENS, HEADS * HD), jnp.float32)
    key_draw = jax.random.normal(key_key, (TOKENS, KV_HEADS * HD), jnp.float32)
    query_draw = jnp.clip(query_draw, -96.0, 96.0)
    key_draw = jnp.clip(key_draw, -96.0, 96.0)
    return (query_draw, key_draw)


def draw_queries(key, part):
    return draw_pair(key)[0].astype(jnp.bfloat16)


def draw_keys(key, part):
    return draw_pair(key)[1].astype(jnp.bfloat16)


def levels(key, extent, cuts, low, largest):
    level = 1.0
    for position, shards_of in cuts:
        draws = jax.random.uniform(jax.random.fold_in(jax.random.fold_in(key, 6), position), (shards_of,), jnp.float32, low / len(cuts), largest / len(cuts))
        level = level * jnp.repeat(jnp.exp(draws), extent[position] // shards_of).reshape((-1,) + (1,) * (len(extent) - 1 - position))
    return level


def split_up(number_of, total, reach, skew):
    portions = [(1 << 20) // math.isqrt(rank ** skew) + 1 for rank in range(2, number_of + 1)]
    spare, holding = total - reach - (number_of - 1), [1] * (number_of - 1)
    while spare > 0:
        movable = [i for i in range(number_of - 1) if holding[i] < reach]
        whole, budget = sum([portions[i] for i in movable]), spare
        for i in movable:
            more = min(reach - holding[i], max(1, budget * portions[i] // whole), spare)
            holding[i] = holding[i] + more
            spare = spare - more
    return np.array([reach] + holding)


def ragged_sizes(rng, count, total, limit, slope):
    if count == 2:
        one = jax.random.randint(rng, (), max(1, total - limit), min(limit, total - 1) + 1)
        return jnp.stack([one, total - one])
    tallies = jnp.asarray(split_up(count, total, limit, slope), jnp.int32)
    twos = (count - 1) // 2
    donor, sink = tallies[1:1 + 2 * twos:2], tallies[2:2 + 2 * twos:2]
    room = jnp.minimum(donor - 1, limit - sink)
    moved = jax.random.randint(jax.random.fold_in(rng, 1), (twos,), 0, 1 << 20) % (room + 1)
    tallies = tallies.at[1:1 + 2 * twos:2].set(donor - moved).at[2:2 + 2 * twos:2].set(sink + moved)
    return tallies[jax.random.permutation(jax.random.fold_in(rng, 2), count)]


def normal_values(own_key, shape, scale, reach, cuts=(), kind=jnp.bfloat16):
    drawn = jax.random.normal(own_key, shape, jnp.float32) * scale
    if len(cuts) > 0:
        drawn = levels(own_key, shape, cuts, -0.22, 0.18) * drawn
    return jnp.clip(drawn, min=-reach, max=reach).astype(kind)


def setup_inputs(seed: int = 0) -> dict:
    key_list = jax.random.split(jax.random.key(seed), 7)
    return {
        "queries": draw_queries(jax.random.fold_in(key_list[6], 71), 0),
        "keys": draw_keys(jax.random.fold_in(key_list[6], 71), 0),
        "values": normal_values(key_list[2], (TOKENS, KV_HEADS * HD), 1.0, 6.0, ((0, 8), (1, 4))),
        "out_weight": normal_values(key_list[3], (HEADS * HD, D), (HEADS * HD) ** -0.5, 0.09375, ((0, 4),)),
        "doc_lengths": ragged_sizes(key_list[4], DOCS, TOKENS, DOC_MOST, 2).astype(jnp.int32),
        "stretch_place": jax.random.permutation(key_list[5], BLOCKS).astype(jnp.int32),
    }


rope_base = 500000.0

def seq_positions(first, count, stretch_place, block_rows):
    row_index = first + jnp.arange(count, dtype=jnp.int32)
    return (stretch_place[row_index // block_rows] * block_rows + row_index % block_rows).astype(jnp.int32)

def documents(positions, doc_lengths):
    ends = jnp.cumsum(doc_lengths).astype(jnp.int32)
    return lax.optimization_barrier(jnp.sum((ends[None, :] <= positions[:, None]).astype(jnp.int32), axis=1))

def rotary(heads_in, positions):
    width = heads_in.shape[-1]
    half = width // 2
    freqs = rope_base ** (-(2.0 / width) * jnp.arange(half, dtype=jnp.float32))
    angles = positions.astype(jnp.float32)[:, None] * freqs[None, :]
    cosine = jnp.cos(angles)[:, None, :]
    sine = jnp.sin(angles)[:, None, :]
    floats = heads_in.astype(jnp.float32)
    first_half = floats[..., :half]
    second_half = floats[..., half:]
    rotated = jnp.concatenate([first_half * cosine - second_half * sine, second_half * cosine + first_half * sine], axis=-1)
    return rotated.astype(jnp.bfloat16)

def reference(queries, keys, values, out_weight, doc_lengths, stretch_place):
    block_rows = TOK_DEV // 2
    positions = seq_positions(0, TOKENS, stretch_place, block_rows)
    document = documents(positions, doc_lengths)
    q_rot = rotary(queries.reshape(TOKENS, HEADS, HD), positions)
    k_rot = rotary(keys.reshape(TOKENS, KV_HEADS, HD), positions)
    value_heads = values.reshape(TOKENS, KV_HEADS, HD)
    order = jnp.zeros((TOKENS,), jnp.int32).at[positions].set(jnp.arange(TOKENS, dtype=jnp.int32))
    q_sorted = q_rot[order]
    k_padded = jnp.concatenate([jnp.zeros((DOC_MOST, KV_HEADS, HD), jnp.bfloat16), k_rot[order]], axis=0)
    v_padded = jnp.concatenate([jnp.zeros((DOC_MOST, KV_HEADS, HD), jnp.bfloat16), value_heads[order]], axis=0)
    doc_sorted = document[order].astype(jnp.int32)
    doc_padded = jnp.concatenate([jnp.full((DOC_MOST,), -1, jnp.int32), doc_sorted], axis=0)
    group = HEADS // KV_HEADS
    scale = 1.0 / math.sqrt(HD)
    window = DOC_MOST + block_rows

    def one_block(index):
        start = (index * block_rows).astype(jnp.int32)
        q_block = lax.dynamic_slice_in_dim(q_sorted, start, block_rows, 0)
        k_block = lax.dynamic_slice_in_dim(k_padded, start, window, 0)
        v_block = lax.dynamic_slice_in_dim(v_padded, start, window, 0)
        q_docs = lax.dynamic_slice_in_dim(doc_sorted, start, block_rows, 0)
        k_docs = lax.dynamic_slice_in_dim(doc_padded, start, window, 0)
        q_pos = start + jnp.arange(block_rows, dtype=jnp.int32)
        k_pos = start - DOC_MOST + jnp.arange(window, dtype=jnp.int32)
        allowed = (k_pos[None, :] <= q_pos[:, None]) & (k_docs[None, :] == q_docs[:, None]) & (k_pos[None, :] >= 0)
        q_float = q_block.astype(jnp.float32).reshape(block_rows, KV_HEADS, group, HD)
        scores = jnp.einsum('tkgd,nkd->kgtn', q_float, k_block.astype(jnp.float32)) * scale
        scores = jnp.where(allowed[None, None], scores, -1e+30)
        row_max = lax.optimization_barrier(jnp.max(scores, axis=-1, keepdims=True))
        weights = jnp.where(allowed[None, None], jnp.exp(scores - row_max), 0.0)
        totals = lax.optimization_barrier(jnp.sum(weights, axis=-1))
        rounded = weights.astype(jnp.bfloat16).astype(jnp.float32)
        mixed = jnp.einsum('kgtn,nkd->tkgd', rounded, v_block.astype(jnp.float32))
        mixed = mixed / jnp.transpose(totals, (2, 0, 1))[..., None]
        return mixed.reshape(block_rows, HEADS * HD)
    sorted_out = lax.map(one_block, jnp.arange(TOKENS // block_rows, dtype=jnp.int32))
    sorted_out = sorted_out.reshape(TOKENS, HEADS * HD)
    attended = sorted_out[positions].astype(jnp.bfloat16)
    return jnp.dot(attended, out_weight, preferred_element_type=jnp.float32).astype(jnp.bfloat16)
```

```python
import functools
import math

import jax
import jax.numpy as jnp
from jax import lax
from jax.experimental import pallas as pl
from jax.experimental.pallas import tpu as pltpu
from jax.sharding import PartitionSpec as P

HD = 128
ROPE_BASE = 500000.0
MASKED = -1e30
FLOOR = -5e29
F32 = jnp.float32
BF16 = jnp.bfloat16
MESH = pl.DeviceIdType.MESH
UNROLL_MOST = 8


def kernel(
    seq_count,
    tensor_count,
    pieces,
    lengths_ref,
    place_ref,
    q_hbm,
    k_hbm,
    v_hbm,
    w_hbm,
    out_ref,
    q_in,
    k_in,
    gk,
    gv,
    qs,
    w_buf,
    attended,
    run_max,
    run_total,
    accum,
    kept,
    send_core,
    recv_core,
    send_chip,
    recv_chip,
    load_sem,
    gather_send,
    gather_recv,
    core_send_sem,
    core_recv_sem,
    chip_send_sem,
    chip_recv_sem,
):
    rows = q_in.shape[0]
    half_rows = rows // 2
    kv_local = k_in.shape[1] // HD
    group = q_in.shape[1] // k_in.shape[1]
    wide = group * rows
    line = seq_count // 2
    chips = tensor_count // 2
    chunk = w_buf.shape[2]
    width = chunk // pieces

    me = lax.axis_index("seq")
    p, y = me // 2, me % 2
    t = lax.axis_index("tensor")
    a, c = t // 2, t % 2
    has_up, has_down = p < line - 1, p > 0
    beside = p * 2 + (1 - y)
    other_core = a * 2 + (1 - c)

    loads = [
        pltpu.make_async_copy(k_hbm, k_in, load_sem.at[0]),
        pltpu.make_async_copy(v_hbm, gv.at[me], load_sem.at[1]),
        pltpu.make_async_copy(q_hbm, q_in, load_sem.at[2]),
    ]
    for load in loads:
        load.start()

    barrier = pltpu.get_barrier_semaphore()

    def greet(where):
        pl.semaphore_signal(barrier, inc=1, device_id=where, device_id_type=MESH)

    greet({"seq": beside})
    greet({"tensor": other_core})
    for i in range(1, chips):
        greet({"tensor": (a + i) % chips * 2 + c})

    @pl.when(has_up)
    def _():
        greet({"seq": me + 2})

    @pl.when(has_down)
    def _():
        greet({"seq": me - 2})

    pl.semaphore_wait(
        barrier, 1 + chips + has_up.astype(jnp.int32) + has_down.astype(jnp.int32)
    )

    def gather_copy(way, block, kind, own=False):
        buf = gk if kind == 0 else gv
        src = v_hbm if own and kind == 1 else buf.at[block]
        target = (me + 2, me - 2, beside)[way]
        return pltpu.make_async_remote_copy(
            src_ref=src,
            dst_ref=buf.at[block],
            send_sem=gather_send.at[way, block // 2, kind],
            recv_sem=gather_recv.at[block, kind],
            device_id={"seq": target},
            device_id_type=MESH,
        )

    def send_own(kind):
        @pl.when(has_up)
        def _():
            gather_copy(0, me, kind, True).start()

        @pl.when(has_down)
        def _():
            gather_copy(1, me, kind, True).start()

        gather_copy(2, me, kind, True).start()

    def arrived(block, kind):
        gather_copy(2, block, kind).wait_recv()

    def forward(place, kind):
        block = place * 2 + y

        @pl.when((place < p) & has_up)
        def _():
            gather_copy(0, block, kind).start()

        @pl.when((place > p) & has_down)
        def _():
            gather_copy(1, block, kind).start()

        gather_copy(2, block, kind).start()

    send_own(1)

    def owner(slot):
        i = slot // 2 + 1
        return (a + i) % chips * 2 + jnp.where(slot % 2 == 0, 1 - c, c)

    weight_loads = []
    for slot in range(tensor_count):
        start = pl.multiple_of(owner(slot) * chunk, 128)
        weight_loads.append(
            pltpu.make_async_copy(
                w_hbm.at[:, pl.ds(start, chunk)], w_buf.at[slot], load_sem.at[3 + slot]
            )
        )

    base0 = place_ref[2 * me] * half_rows
    base1 = place_ref[2 * me + 1] * half_rows

    def positions(shape, axis):
        row = lax.broadcasted_iota(jnp.int32, shape, axis) % rows
        return jnp.where(row < half_rows, base0 + row, base1 + row - half_rows)

    lane = lax.broadcasted_iota(jnp.int32, (rows, HD), 1)
    freq = jnp.exp((lane % (HD // 2)).astype(F32) * (-2.0 / HD * math.log(ROPE_BASE)))
    angle = positions((rows, HD), 0).astype(F32) * freq
    cosine = jnp.cos(angle)
    sine = jnp.where(lane < HD // 2, -jnp.sin(angle), jnp.sin(angle))

    def rotate(block):
        floats = block.astype(F32)
        return (floats * cosine + pltpu.roll(floats, HD // 2, 1) * sine).astype(BF16)

    loads[0].wait()
    for h in range(kv_local):
        gk[me, :, h * HD : (h + 1) * HD] = rotate(k_in[:, h * HD : (h + 1) * HD])
    send_own(0)
    for load in weight_loads:
        load.start()

    loads[2].wait()
    for h in range(kv_local):
        for g in range(group):
            column = (h * group + g) * HD
            qs[h, g * rows : (g + 1) * rows, :] = rotate(q_in[:, column : column + HD])

    last = positions((1, wide), 1)
    first = jnp.zeros((1, wide), jnp.int32)
    end = jnp.int32(0)
    for i in range(lengths_ref.shape[0]):
        end = end + lengths_ref[i]
        first = jnp.maximum(first, jnp.where(end <= last, end, 0))

    run_max[...] = jnp.full_like(run_max, FLOOR)
    run_total[...] = jnp.zeros_like(run_total)
    accum[...] = jnp.zeros_like(accum)
    scale = math.log2(math.e) / math.sqrt(HD)

    def attend(block):
        row = lax.broadcasted_iota(jnp.int32, (half_rows, wide), 0)
        allowed = []
        for j in range(2):
            base = place_ref[2 * block + j] * half_rows
            allowed.append((row >= first - base) & (row <= last - base))
        for h in range(kv_local):
            key = gk[block, :, h * HD : (h + 1) * HD]
            value = gv[block, :, h * HD : (h + 1) * HD]
            scores = lax.dot_general(
                key, qs[h], (((1,), (1,)), ((), ())), preferred_element_type=F32
            )
            scores = jnp.concatenate(
                [
                    jnp.where(allowed[j], scores[j * half_rows : (j + 1) * half_rows], MASKED)
                    for j in range(2)
                ],
                axis=0,
            )
            old = run_max[h]
            new = jnp.maximum(old, jnp.max(scores, axis=0, keepdims=True))
            weights = jnp.exp2((scores - new) * scale)
            factor = jnp.exp2((old - new) * scale)
            run_max[h] = new
            run_total[h] = run_total[h] * factor + jnp.sum(weights, axis=0, keepdims=True)
            accum[h] = accum[h] * factor + lax.dot_general(
                value,
                weights.astype(BF16),
                (((0,), (0,)), ((), ())),
                preferred_element_type=F32,
            )

    loads[1].wait()
    attend(me)

    near = jnp.minimum(p, line - 1 - p)

    def nth_place(k):
        apart = (k + 1) // 2
        both = jnp.where(k % 2 == 1, p - apart, p + apart)
        single = jnp.where(p < line - 1 - p, p + (k - near), p - (k - near))
        return jnp.where(k <= 2 * near, both, single)

    def step(k):
        place = nth_place(k)
        for kind in (1, 0):
            arrived(place * 2 + y, kind)
            forward(place, kind)
        attend(place * 2 + y)
        across = nth_place(k - 1) * 2 + (1 - y)
        for kind in (1, 0):
            arrived(across, kind)
        attend(across)

    def repeat(low, high, body):
        if high - low < UNROLL_MOST:
            for k in range(low, high):
                body(jnp.int32(k))
        else:

            def one(k, carry):
                body(k)
                return carry

            lax.fori_loop(low, high, one, 0)

    repeat(1, line, step)
    across = nth_place(jnp.int32(line - 1)) * 2 + (1 - y)
    for kind in (1, 0):
        arrived(across, kind)
    attend(across)

    for h in range(kv_local):
        mixed = (accum[h] * (1.0 / run_total[h])).T.astype(BF16)
        for g in range(group):
            column = (h * group + g) * HD
            attended[:, column : column + HD] = mixed[g * rows : (g + 1) * rows]

    def partial_sum(slot, j):
        return jnp.dot(
            attended[...],
            w_buf[slot, :, j * width : (j + 1) * width],
            preferred_element_type=F32,
        )

    def core_copy(i, j):
        return pltpu.make_async_remote_copy(
            src_ref=send_core.at[i, j],
            dst_ref=recv_core.at[i, j],
            send_sem=core_send_sem.at[i, j],
            recv_sem=core_recv_sem.at[i, j],
            device_id={"tensor": other_core},
            device_id_type=MESH,
        )

    def chip_copy(i, j):
        return pltpu.make_async_remote_copy(
            src_ref=send_chip.at[i, j],
            dst_ref=recv_chip.at[i, j],
            send_sem=chip_send_sem.at[i, j],
            recv_sem=chip_recv_sem.at[i, j],
            device_id={"tensor": (a + i + 1) % chips * 2 + c},
            device_id_type=MESH,
        )

    def pass_on(i, j):
        core_copy(i, j).wait_recv()
        send_chip[i, j] = (kept[i, j] + recv_core[i, j].astype(F32)).astype(BF16)
        chip_copy(i, j).start()

    waiting = []
    for i in range(chips):
        for j in range(pieces):
            if j == 0:
                weight_loads[2 * i].wait()
            send_core[i, j] = partial_sum(2 * i, j).astype(BF16)
            core_copy(i, j).start()
            if j == 0:
                weight_loads[2 * i + 1].wait()
            kept[i, j] = partial_sum(2 * i + 1, j)
            if waiting:
                pass_on(*waiting.pop())
            if i < chips - 1:
                waiting.append((i, j))
    for j in range(pieces):
        core_copy(chips - 1, j).wait_recv()
        total = kept[chips - 1, j] + recv_core[chips - 1, j].astype(F32)
        for i in range(chips - 1):
            chip_copy(i, j).wait_recv()
            total = total + recv_chip[i, j].astype(F32)
        out_ref[:, j * width : (j + 1) * width] = total.astype(BF16)

    def drain(place):
        block = place * 2 + y
        for kind in (1, 0):

            @pl.when((place <= p) & has_up)
            def _():
                gather_copy(0, block, kind).wait_send()

            @pl.when((place >= p) & has_down)
            def _():
                gather_copy(1, block, kind).wait_send()

            gather_copy(2, block, kind).wait_send()

    repeat(0, line, drain)
    for i in range(chips):
        for j in range(pieces):
            core_copy(i, j).wait_send()
            if i < chips - 1:
                chip_copy(i, j).wait_send()


def solution(mesh):
    seq_count, tensor_count = mesh.shape["seq"], mesh.shape["tensor"]

    def body(queries, keys, values, out_weight, doc_lengths, stretch_place):
        rows, q_width = queries.shape
        kv_width = keys.shape[1]
        model = out_weight.shape[1]
        kv_local = kv_width // HD
        wide = q_width // kv_width * rows
        chips = tensor_count // 2
        chunk = model // tensor_count
        pieces = max(1, chunk // 256)
        width = chunk // pieces
        smem = pl.BlockSpec(memory_space=pltpu.SMEM)
        anywhere = pl.BlockSpec(memory_space=pl.ANY)
        dma = pltpu.SemaphoreType.DMA
        return pl.pallas_call(
            functools.partial(kernel, seq_count, tensor_count, pieces),
            out_shape=jax.ShapeDtypeStruct((rows, chunk), BF16),
            in_specs=[smem, smem] + [anywhere] * 4,
            out_specs=pl.BlockSpec(memory_space=pltpu.VMEM),
            scratch_shapes=[
                pltpu.VMEM((rows, q_width), BF16),
                pltpu.VMEM((rows, kv_width), BF16),
                pltpu.VMEM((seq_count, rows, kv_width), BF16),
                pltpu.VMEM((seq_count, rows, kv_width), BF16),
                pltpu.VMEM((kv_local, wide, HD), BF16),
                pltpu.VMEM((tensor_count, q_width, chunk), BF16),
                pltpu.VMEM((rows, q_width), BF16),
                pltpu.VMEM((kv_local, 1, wide), F32),
                pltpu.VMEM((kv_local, 1, wide), F32),
                pltpu.VMEM((kv_local, HD, wide), F32),
                pltpu.VMEM((chips, pieces, rows, width), F32),
                pltpu.VMEM((chips, pieces, rows, width), BF16),
                pltpu.VMEM((chips, pieces, rows, width), BF16),
                pltpu.VMEM((chips - 1, pieces, rows, width), BF16),
                pltpu.VMEM((chips - 1, pieces, rows, width), BF16),
                dma((3 + tensor_count,)),
                dma((3, seq_count // 2, 2)),
                dma((seq_count, 2)),
                dma((chips, pieces)),
                dma((chips, pieces)),
                dma((chips - 1, pieces)),
                dma((chips - 1, pieces)),
            ],
            compiler_params=pltpu.CompilerParams(collective_id=0, has_side_effects=True),
            name="attention_layer",
        )(doc_lengths, stretch_place, queries, keys, values, out_weight)

    in_specs = (
        P("seq", "tensor"),
        P("seq", "tensor"),
        P("seq", "tensor"),
        P("tensor", None),
        P(),
        P(),
    )
    return jax.shard_map(
        body, mesh=mesh, in_specs=in_specs, out_specs=P("seq", "tensor"), check_vma=False
    )
```

```python
import functools
import math

import jax
import jax.numpy as jnp
from jax import lax
from jax.experimental import pallas as pl
from jax.experimental.pallas import tpu as pltpu
from jax.sharding import PartitionSpec as P

HD = 128
ROPE_BASE = 500000.0
MASKED = -1e30
FLOOR = -5e29
F32 = jnp.float32
BF16 = jnp.bfloat16
MESH = pl.DeviceIdType.MESH
UNROLL_MOST = 8
DIRECT_MOST = 2
VMEM_LIMIT = 50 * 1024 * 1024


def kernel(
    seq_count,
    tensor_count,
    pieces,
    lengths_ref,
    place_ref,
    q_hbm,
    k_hbm,
    v_hbm,
    w_hbm,
    out_ref,
    q_in,
    k_in,
    gk,
    gv,
    qs,
    w_buf,
    attended,
    run_max,
    run_total,
    accum,
    kept,
    send_core,
    recv_core,
    send_chip,
    recv_chip,
    load_sem,
    gather_send,
    gather_recv,
    core_send_sem,
    core_recv_sem,
    chip_send_sem,
    chip_recv_sem,
):
    rows = q_in.shape[0]
    half_rows = rows // 2
    kv_local = k_in.shape[1] // HD
    group = q_in.shape[1] // k_in.shape[1]
    wide = group * rows
    line = seq_count // 2
    chips = tensor_count // 2
    chunk = w_buf.shape[2]
    width = chunk // pieces

    me = lax.axis_index("seq")
    p, y = me // 2, me % 2
    t = lax.axis_index("tensor")
    a, c = t // 2, t % 2
    has_up, has_down = p < line - 1, p > 0
    direct = 2 < line <= DIRECT_MOST
    from_end = lambda place: (place == 0) | (place == line - 1)
    beside = p * 2 + (1 - y)
    other_core = a * 2 + (1 - c)

    loads = [
        pltpu.make_async_copy(k_hbm, k_in, load_sem.at[0]),
        pltpu.make_async_copy(v_hbm, gv.at[me], load_sem.at[1]),
        pltpu.make_async_copy(q_hbm, q_in, load_sem.at[2]),
    ]
    for load in loads:
        load.start()

    barrier = pltpu.get_barrier_semaphore()

    def greet(where):
        pl.semaphore_signal(barrier, inc=1, device_id=where, device_id_type=MESH)

    greet({"seq": beside})
    greet({"tensor": other_core})
    for i in range(1, chips):
        greet({"tensor": (a + i) % chips * 2 + c})

    @pl.when(has_up)
    def _():
        greet({"seq": me + 2})

    @pl.when(has_down)
    def _():
        greet({"seq": me - 2})

    greeted = 1 + chips + has_up.astype(jnp.int32) + has_down.astype(jnp.int32)
    if direct:
        for apart in range(2, line):

            @pl.when(p + apart < line)
            def _():
                @pl.when((p == 0) | (p + apart == line - 1))
                def _():
                    greet({"seq": me + 2 * apart})

            @pl.when(p - apart >= 0)
            def _():
                @pl.when((p == line - 1) | (p - apart == 0))
                def _():
                    greet({"seq": me - 2 * apart})

            above = (p + apart < line) & ((p == 0) | (p + apart == line - 1))
            below = (p - apart >= 0) & ((p == line - 1) | (p - apart == 0))
            greeted = greeted + above.astype(jnp.int32) + below.astype(jnp.int32)
    pl.semaphore_wait(barrier, greeted)

    def far_target(apart):
        return me + jnp.where(p == 0, 2 * apart, -2 * apart)

    def gather_copy(way, block, kind, own=False):
        buf = gk if kind == 0 else gv
        src = v_hbm if own and kind == 1 else buf.at[block]
        target = (me + 2, me - 2, beside)[way] if way < 3 else far_target(way - 1)
        return pltpu.make_async_remote_copy(
            src_ref=src,
            dst_ref=buf.at[block],
            send_sem=gather_send.at[way, block // 2, kind],
            recv_sem=gather_recv.at[block, kind],
            device_id={"seq": target},
            device_id_type=MESH,
        )

    def send_own(kind):
        if direct:
            for apart in range(line - 1, 1, -1):

                @pl.when(from_end(p))
                def _():
                    gather_copy(apart + 1, me, kind, True).start()

        @pl.when(has_up)
        def _():
            gather_copy(0, me, kind, True).start()

        @pl.when(has_down)
        def _():
            gather_copy(1, me, kind, True).start()

        gather_copy(2, me, kind, True).start()

    def arrived(block, kind):
        gather_copy(2, block, kind).wait_recv()

    def forward(place, kind):
        block = place * 2 + y

        keep = from_end(place) if direct else place != place

        @pl.when((place < p) & has_up & ~keep)
        def _():
            gather_copy(0, block, kind).start()

        @pl.when((place > p) & has_down & ~keep)
        def _():
            gather_copy(1, block, kind).start()

        gather_copy(2, block, kind).start()

    send_own(1)

    def owner(slot):
        i = slot // 2 + 1
        return (a + i) % chips * 2 + jnp.where(slot % 2 == 0, 1 - c, c)

    weight_loads = []
    for slot in range(tensor_count):
        start = pl.multiple_of(owner(slot) * chunk, 128)
        weight_loads.append(
            pltpu.make_async_copy(
                w_hbm.at[:, pl.ds(start, chunk)], w_buf.at[slot], load_sem.at[3 + slot]
            )
        )

    base0 = place_ref[2 * me] * half_rows
    base1 = place_ref[2 * me + 1] * half_rows

    def positions(shape, axis):
        row = lax.broadcasted_iota(jnp.int32, shape, axis) % rows
        return jnp.where(row < half_rows, base0 + row, base1 + row - half_rows)

    lane = lax.broadcasted_iota(jnp.int32, (rows, HD), 1)
    freq = jnp.exp((lane % (HD // 2)).astype(F32) * (-2.0 / HD * math.log(ROPE_BASE)))
    angle = positions((rows, HD), 0).astype(F32) * freq
    cosine = jnp.cos(angle)
    sine = jnp.where(lane < HD // 2, -jnp.sin(angle), jnp.sin(angle))

    def rotate(block):
        floats = block.astype(F32)
        return (floats * cosine + pltpu.roll(floats, HD // 2, 1) * sine).astype(BF16)

    loads[0].wait()
    for h in range(kv_local):
        gk[me, :, h * HD : (h + 1) * HD] = rotate(k_in[:, h * HD : (h + 1) * HD])
    send_own(0)
    for load in weight_loads:
        load.start()

    loads[2].wait()
    for h in range(kv_local):
        for g in range(group):
            column = (h * group + g) * HD
            qs[h, g * rows : (g + 1) * rows, :] = rotate(q_in[:, column : column + HD])

    last = positions((1, wide), 1)
    first = jnp.zeros((1, wide), jnp.int32)
    end = jnp.int32(0)
    for i in range(lengths_ref.shape[0]):
        end = end + lengths_ref[i]
        first = jnp.maximum(first, jnp.where(end <= last, end, 0))

    run_max[...] = jnp.full_like(run_max, FLOOR)
    run_total[...] = jnp.zeros_like(run_total)
    accum[...] = jnp.zeros_like(accum)
    scale = math.log2(math.e) / math.sqrt(HD)

    def attend(block):
        row = lax.broadcasted_iota(jnp.int32, (half_rows, wide), 0)
        allowed = []
        for j in range(2):
            base = place_ref[2 * block + j] * half_rows
            allowed.append((row >= first - base) & (row <= last - base))
        for h in range(kv_local):
            key = gk[block, :, h * HD : (h + 1) * HD]
            value = gv[block, :, h * HD : (h + 1) * HD]
            scores = lax.dot_general(
                key, qs[h], (((1,), (1,)), ((), ())), preferred_element_type=F32
            )
            scores = jnp.concatenate(
                [
                    jnp.where(allowed[j], scores[j * half_rows : (j + 1) * half_rows], MASKED)
                    for j in range(2)
                ],
                axis=0,
            )
            old = run_max[h]
            new = jnp.maximum(old, jnp.max(scores, axis=0, keepdims=True))
            weights = jnp.exp2((scores - new) * scale)
            factor = jnp.exp2((old - new) * scale)
            run_max[h] = new
            run_total[h] = run_total[h] * factor + jnp.sum(weights, axis=0, keepdims=True)
            accum[h] = accum[h] * factor + lax.dot_general(
                value,
                weights.astype(BF16),
                (((0,), (0,)), ((), ())),
                preferred_element_type=F32,
            )

    loads[1].wait()
    attend(me)

    near = jnp.minimum(p, line - 1 - p)

    def nth_place(k):
        apart = (k + 1) // 2
        both = jnp.where(k % 2 == 1, p - apart, p + apart)
        single = jnp.where(p < line - 1 - p, p + (k - near), p - (k - near))
        return jnp.where(k <= 2 * near, both, single)

    def attend_across(k):
        across = nth_place(k) * 2 + (1 - y)
        for kind in (1, 0):
            arrived(across, kind)
        attend(across)

    def step(k):
        place = nth_place(k)
        for kind in (1, 0):
            arrived(place * 2 + y, kind)
            forward(place, kind)
        attend(place * 2 + y)

        @pl.when(k > 1)
        def _():
            attend_across(k - 2)

    def repeat(low, high, body):
        if high - low < UNROLL_MOST:
            for k in range(low, high):
                body(jnp.int32(k))
        else:

            def one(k, carry):
                body(k)
                return carry

            lax.fori_loop(low, high, one, 0)

    repeat(1, line, step)
    for k in range(max(0, line - 2), line):
        attend_across(jnp.int32(k))

    for h in range(kv_local):
        mixed = (accum[h] * (1.0 / run_total[h])).T.astype(BF16)
        for g in range(group):
            column = (h * group + g) * HD
            attended[:, column : column + HD] = mixed[g * rows : (g + 1) * rows]

    def partial_sum(slot, j):
        return jnp.dot(
            attended[...],
            w_buf[slot, :, j * width : (j + 1) * width],
            preferred_element_type=F32,
        )

    def core_copy(i, j):
        return pltpu.make_async_remote_copy(
            src_ref=send_core.at[i, j],
            dst_ref=recv_core.at[i, j],
            send_sem=core_send_sem.at[i, j],
            recv_sem=core_recv_sem.at[i, j],
            device_id={"tensor": other_core},
            device_id_type=MESH,
        )

    def chip_copy(i, j):
        return pltpu.make_async_remote_copy(
            src_ref=send_chip.at[i, j],
            dst_ref=recv_chip.at[i, j],
            send_sem=chip_send_sem.at[i, j],
            recv_sem=chip_recv_sem.at[i, j],
            device_id={"tensor": (a + i + 1) % chips * 2 + c},
            device_id_type=MESH,
        )

    def pass_on(i, j):
        core_copy(i, j).wait_recv()
        send_chip[i, j] = (kept[i, j] + recv_core[i, j].astype(F32)).astype(BF16)
        chip_copy(i, j).start()

    waiting = []
    for i in range(chips):
        for j in range(pieces):
            if j == 0:
                weight_loads[2 * i].wait()
            send_core[i, j] = partial_sum(2 * i, j).astype(BF16)
            core_copy(i, j).start()
            if j == 0:
                weight_loads[2 * i + 1].wait()
            kept[i, j] = partial_sum(2 * i + 1, j)
            if waiting:
                pass_on(*waiting.pop())
            if i < chips - 1:
                waiting.append((i, j))
    for j in range(pieces):
        core_copy(chips - 1, j).wait_recv()
        total = kept[chips - 1, j] + recv_core[chips - 1, j].astype(F32)
        for i in range(chips - 1):
            chip_copy(i, j).wait_recv()
            total = total + recv_chip[i, j].astype(F32)
        out_ref[:, j * width : (j + 1) * width] = total

    def drain(place):
        block = place * 2 + y
        keep = from_end(place) & (place != p) if direct else place != place
        for kind in (1, 0):

            @pl.when((place <= p) & has_up & ~keep)
            def _():
                gather_copy(0, block, kind).wait_send()

            @pl.when((place >= p) & has_down & ~keep)
            def _():
                gather_copy(1, block, kind).wait_send()

            gather_copy(2, block, kind).wait_send()

    repeat(0, line, drain)
    if direct:
        for apart in range(line - 1, 1, -1):
            for kind in (1, 0):

                @pl.when(from_end(p))
                def _():
                    gather_copy(apart + 1, me, kind).wait_send()

    for i in range(chips):
        for j in range(pieces):
            core_copy(i, j).wait_send()
            if i < chips - 1:
                chip_copy(i, j).wait_send()


def solution(mesh):
    seq_count, tensor_count = mesh.shape["seq"], mesh.shape["tensor"]

    def body(queries, keys, values, out_weight, doc_lengths, stretch_place):
        rows, q_width = queries.shape
        kv_width = keys.shape[1]
        model = out_weight.shape[1]
        kv_local = kv_width // HD
        wide = q_width // kv_width * rows
        chips = tensor_count // 2
        chunk = model // tensor_count
        pieces = max(1, chunk // 256)
        width = chunk // pieces
        smem = pl.BlockSpec(memory_space=pltpu.SMEM)
        anywhere = pl.BlockSpec(memory_space=pltpu.HBM)
        dma = pltpu.SemaphoreType.DMA
        total = pl.pallas_call(
            functools.partial(kernel, seq_count, tensor_count, pieces),
            out_shape=jax.ShapeDtypeStruct((rows, chunk), F32),
            in_specs=[smem, smem] + [anywhere] * 4,
            out_specs=pl.BlockSpec(memory_space=pltpu.VMEM),
            scratch_shapes=[
                pltpu.VMEM((rows, q_width), BF16),
                pltpu.VMEM((rows, kv_width), BF16),
                pltpu.VMEM((seq_count, rows, kv_width), BF16),
                pltpu.VMEM((seq_count, rows, kv_width), BF16),
                pltpu.VMEM((kv_local, wide, HD), BF16),
                pltpu.VMEM((tensor_count, q_width, chunk), BF16),
                pltpu.VMEM((rows, q_width), BF16),
                pltpu.VMEM((kv_local, 1, wide), F32),
                pltpu.VMEM((kv_local, 1, wide), F32),
                pltpu.VMEM((kv_local, HD, wide), F32),
                pltpu.VMEM((chips, pieces, rows, width), F32),
                pltpu.VMEM((chips, pieces, rows, width), BF16),
                pltpu.VMEM((chips, pieces, rows, width), BF16),
                pltpu.VMEM((chips - 1, pieces, rows, width), BF16),
                pltpu.VMEM((chips - 1, pieces, rows, width), BF16),
                dma((3 + tensor_count,)),
                dma((2 + max(1, min(seq_count // 2, DIRECT_MOST) - 1), seq_count // 2, 2)),
                dma((seq_count, 2)),
                dma((chips, pieces)),
                dma((chips, pieces)),
                dma((chips - 1, pieces)),
                dma((chips - 1, pieces)),
            ],
            compiler_params=pltpu.CompilerParams(
                collective_id=0, has_side_effects=True, vmem_limit_bytes=VMEM_LIMIT
            ),
            name="attention_layer",
        )(*[
            pltpu.with_memory_space_constraint(x, pltpu.HBM)
            for x in (doc_lengths, stretch_place, queries, keys, values, out_weight)
        ])
        return total.astype(BF16)

    in_specs = (
        P("seq", "tensor"),
        P("seq", "tensor"),
        P("seq", "tensor"),
        P("tensor", None),
        P(),
        P(),
    )
    return jax.shard_map(
        body, mesh=mesh, in_specs=in_specs, out_specs=P("seq", "tensor"), check_vma=False
    )
```

```python
import functools
import math

import jax
import jax.numpy as jnp
from jax import lax
from jax.experimental import pallas as pl
from jax.experimental.pallas import tpu as pltpu
from jax.sharding import PartitionSpec as P

HD = 128
ROPE_BASE = 500000.0
MASKED = -1e30
FLOOR = -5e29
F32 = jnp.float32
BF16 = jnp.bfloat16
MESH = pl.DeviceIdType.MESH
UNROLL_MOST = 8
DIRECT_MOST = 2
VMEM_LIMIT = 50 * 1024 * 1024


def kernel(
    seq_count,
    tensor_count,
    pieces,
    lengths_ref,
    place_ref,
    q_hbm,
    k_hbm,
    v_hbm,
    w_hbm,
    out_ref,
    q_in,
    k_in,
    gk,
    gv,
    qs,
    w_buf,
    attended,
    run_max,
    run_total,
    accum,
    kept,
    send_core,
    recv_core,
    send_chip,
    recv_chip,
    load_sem,
    gather_send,
    gather_recv,
    core_send_sem,
    core_recv_sem,
    chip_send_sem,
    chip_recv_sem,
):
    rows = q_in.shape[0]
    half_rows = rows // 2
    kv_local = k_in.shape[1] // HD
    group = q_in.shape[1] // k_in.shape[1]
    wide = group * rows
    line = seq_count // 2
    chips = tensor_count // 2
    chunk = w_buf.shape[2]
    width = chunk // pieces

    me = lax.axis_index("seq")
    p, y = me // 2, me % 2
    t = lax.axis_index("tensor")
    a, c = t // 2, t % 2
    has_up, has_down = p < line - 1, p > 0
    direct = 2 < line <= DIRECT_MOST
    from_end = lambda place: (place == 0) | (place == line - 1)
    beside = p * 2 + (1 - y)
    other_core = a * 2 + (1 - c)

    loads = [
        pltpu.make_async_copy(k_hbm, k_in, load_sem.at[0]),
        pltpu.make_async_copy(v_hbm, gv.at[me], load_sem.at[1]),
        pltpu.make_async_copy(q_hbm, q_in, load_sem.at[2]),
    ]
    for load in loads:
        load.start()

    barrier = pltpu.get_barrier_semaphore()

    def greet(where):
        pl.semaphore_signal(barrier, inc=1, device_id=where, device_id_type=MESH)

    greet({"seq": beside})
    greet({"tensor": other_core})
    for i in range(1, chips):
        greet({"tensor": (a + i) % chips * 2 + c})

    @pl.when(has_up)
    def _():
        greet({"seq": me + 2})

    @pl.when(has_down)
    def _():
        greet({"seq": me - 2})

    greeted = 1 + chips + has_up.astype(jnp.int32) + has_down.astype(jnp.int32)
    if direct:
        for apart in range(2, line):

            @pl.when(p + apart < line)
            def _():
                @pl.when((p == 0) | (p + apart == line - 1))
                def _():
                    greet({"seq": me + 2 * apart})

            @pl.when(p - apart >= 0)
            def _():
                @pl.when((p == line - 1) | (p - apart == 0))
                def _():
                    greet({"seq": me - 2 * apart})

            above = (p + apart < line) & ((p == 0) | (p + apart == line - 1))
            below = (p - apart >= 0) & ((p == line - 1) | (p - apart == 0))
            greeted = greeted + above.astype(jnp.int32) + below.astype(jnp.int32)
    pl.semaphore_wait(barrier, greeted)

    def far_target(apart):
        return me + jnp.where(p == 0, 2 * apart, -2 * apart)

    def gather_copy(way, block, kind, own=False):
        buf = gk if kind == 0 else gv
        src = v_hbm if own and kind == 1 else buf.at[block]
        target = (me + 2, me - 2, beside)[way] if way < 3 else far_target(way - 1)
        return pltpu.make_async_remote_copy(
            src_ref=src,
            dst_ref=buf.at[block],
            send_sem=gather_send.at[way, block // 2, kind],
            recv_sem=gather_recv.at[block, kind],
            device_id={"seq": target},
            device_id_type=MESH,
        )

    def send_own(kind):
        if direct:
            for apart in range(line - 1, 1, -1):

                @pl.when(from_end(p))
                def _():
                    gather_copy(apart + 1, me, kind, True).start()

        @pl.when(has_up)
        def _():
            gather_copy(0, me, kind, True).start()

        @pl.when(has_down)
        def _():
            gather_copy(1, me, kind, True).start()

        gather_copy(2, me, kind, True).start()

    def arrived(block, kind):
        gather_copy(2, block, kind).wait_recv()

    def forward(place, kind):
        block = place * 2 + y

        keep = from_end(place) if direct else place != place

        @pl.when((place < p) & has_up & ~keep)
        def _():
            gather_copy(0, block, kind).start()

        @pl.when((place > p) & has_down & ~keep)
        def _():
            gather_copy(1, block, kind).start()

        gather_copy(2, block, kind).start()

    send_own(1)

    def owner(slot):
        i = slot // 2 + 1
        return (a + i) % chips * 2 + jnp.where(slot % 2 == 0, 1 - c, c)

    weight_loads = []
    for slot in range(tensor_count):
        start = pl.multiple_of(owner(slot) * chunk, 128)
        weight_loads.append(
            pltpu.make_async_copy(
                w_hbm.at[:, pl.ds(start, chunk)], w_buf.at[slot], load_sem.at[3 + slot]
            )
        )

    base0 = place_ref[2 * me] * half_rows
    base1 = place_ref[2 * me + 1] * half_rows

    def positions(shape, axis):
        row = lax.broadcasted_iota(jnp.int32, shape, axis) % rows
        return jnp.where(row < half_rows, base0 + row, base1 + row - half_rows)

    lane = lax.broadcasted_iota(jnp.int32, (rows, HD), 1)
    freq = jnp.exp((lane % (HD // 2)).astype(F32) * (-2.0 / HD * math.log(ROPE_BASE)))
    angle = positions((rows, HD), 0).astype(F32) * freq
    cosine = jnp.cos(angle)
    sine = jnp.where(lane < HD // 2, -jnp.sin(angle), jnp.sin(angle))

    def rotate(block):
        floats = block.astype(F32)
        return (floats * cosine + pltpu.roll(floats, HD // 2, 1) * sine).astype(BF16)

    loads[0].wait()
    for h in range(kv_local):
        gk[me, :, h * HD : (h + 1) * HD] = rotate(k_in[:, h * HD : (h + 1) * HD])
    send_own(0)
    for load in weight_loads:
        load.start()

    near = jnp.minimum(p, line - 1 - p)

    def nth_place(k):
        apart = (k + 1) // 2
        both = jnp.where(k % 2 == 1, p - apart, p + apart)
        single = jnp.where(p < line - 1 - p, p + (k - near), p - (k - near))
        return jnp.where(k <= 2 * near, both, single)

    def relay(k):
        place = nth_place(k)
        for kind in (1, 0):
            arrived(place * 2 + y, kind)
            forward(place, kind)

    for k in range(1, min(3, line)):
        relay(jnp.int32(k))

    loads[2].wait()
    for h in range(kv_local):
        for g in range(group):
            column = (h * group + g) * HD
            qs[h, g * rows : (g + 1) * rows, :] = rotate(q_in[:, column : column + HD])

    last = positions((1, wide), 1)
    first = jnp.zeros((1, wide), jnp.int32)
    end = jnp.int32(0)
    for i in range(lengths_ref.shape[0]):
        end = end + lengths_ref[i]
        first = jnp.maximum(first, jnp.where(end <= last, end, 0))

    run_max[...] = jnp.full_like(run_max, FLOOR)
    run_total[...] = jnp.zeros_like(run_total)
    accum[...] = jnp.zeros_like(accum)
    scale = math.log2(math.e) / math.sqrt(HD)

    def attend(block):
        row = lax.broadcasted_iota(jnp.int32, (half_rows, wide), 0)
        allowed = []
        for j in range(2):
            base = place_ref[2 * block + j] * half_rows
            allowed.append((row >= first - base) & (row <= last - base))
        for h in range(kv_local):
            key = gk[block, :, h * HD : (h + 1) * HD]
            value = gv[block, :, h * HD : (h + 1) * HD]
            scores = lax.dot_general(
                key, qs[h], (((1,), (1,)), ((), ())), preferred_element_type=F32
            )
            scores = jnp.concatenate(
                [
                    jnp.where(allowed[j], scores[j * half_rows : (j + 1) * half_rows], MASKED)
                    for j in range(2)
                ],
                axis=0,
            )
            old = run_max[h]
            new = jnp.maximum(old, jnp.max(scores, axis=0, keepdims=True))
            weights = jnp.exp2((scores - new) * scale)
            factor = jnp.exp2((old - new) * scale)
            run_max[h] = new
            run_total[h] = run_total[h] * factor + jnp.sum(weights, axis=0, keepdims=True)
            accum[h] = accum[h] * factor + lax.dot_general(
                value,
                weights.astype(BF16),
                (((0,), (0,)), ((), ())),
                preferred_element_type=F32,
            )

    loads[1].wait()
    attend(me)

    def attend_across(k):
        across = nth_place(k) * 2 + (1 - y)
        for kind in (1, 0):
            arrived(across, kind)
        attend(across)

    def step(k):
        attend(nth_place(k) * 2 + y)

        @pl.when(k + 2 < line)
        def _():
            relay(k + 2)

        @pl.when(k > 1)
        def _():
            attend_across(k - 2)

    def repeat(low, high, body):
        if high - low < UNROLL_MOST:
            for k in range(low, high):
                body(jnp.int32(k))
        else:

            def one(k, carry):
                body(k)
                return carry

            lax.fori_loop(low, high, one, 0)

    repeat(1, line, step)
    for k in range(max(0, line - 2), line):
        attend_across(jnp.int32(k))

    for h in range(kv_local):
        mixed = (accum[h] * (1.0 / run_total[h])).T.astype(BF16)
        for g in range(group):
            column = (h * group + g) * HD
            attended[:, column : column + HD] = mixed[g * rows : (g + 1) * rows]

    def partial_sum(slot, j):
        return jnp.dot(
            attended[...],
            w_buf[slot, :, j * width : (j + 1) * width],
            preferred_element_type=F32,
        )

    def core_copy(i, j):
        return pltpu.make_async_remote_copy(
            src_ref=send_core.at[i, j],
            dst_ref=recv_core.at[i, j],
            send_sem=core_send_sem.at[i, j],
            recv_sem=core_recv_sem.at[i, j],
            device_id={"tensor": other_core},
            device_id_type=MESH,
        )

    def chip_copy(i, j):
        return pltpu.make_async_remote_copy(
            src_ref=send_chip.at[i, j],
            dst_ref=recv_chip.at[i, j],
            send_sem=chip_send_sem.at[i, j],
            recv_sem=chip_recv_sem.at[i, j],
            device_id={"tensor": (a + i + 1) % chips * 2 + c},
            device_id_type=MESH,
        )

    def pass_on(i, j):
        core_copy(i, j).wait_recv()
        send_chip[i, j] = (kept[i, j] + recv_core[i, j].astype(F32)).astype(BF16)
        chip_copy(i, j).start()

    waiting = []
    for i in range(chips):
        for j in range(pieces):
            if j == 0:
                weight_loads[2 * i].wait()
            send_core[i, j] = partial_sum(2 * i, j).astype(BF16)
            core_copy(i, j).start()
            if j == 0:
                weight_loads[2 * i + 1].wait()
            kept[i, j] = partial_sum(2 * i + 1, j)
            if waiting:
                pass_on(*waiting.pop())
            if i < chips - 1:
                waiting.append((i, j))
    for j in range(pieces):
        core_copy(chips - 1, j).wait_recv()
        total = kept[chips - 1, j] + recv_core[chips - 1, j].astype(F32)
        for i in range(chips - 1):
            chip_copy(i, j).wait_recv()
            total = total + recv_chip[i, j].astype(F32)
        out_ref[:, j * width : (j + 1) * width] = total

    def drain(place):
        block = place * 2 + y
        keep = from_end(place) & (place != p) if direct else place != place
        for kind in (1, 0):

            @pl.when((place <= p) & has_up & ~keep)
            def _():
                gather_copy(0, block, kind).wait_send()

            @pl.when((place >= p) & has_down & ~keep)
            def _():
                gather_copy(1, block, kind).wait_send()

            gather_copy(2, block, kind).wait_send()

    repeat(0, line, drain)
    if direct:
        for apart in range(line - 1, 1, -1):
            for kind in (1, 0):

                @pl.when(from_end(p))
                def _():
                    gather_copy(apart + 1, me, kind).wait_send()

    for i in range(chips):
        for j in range(pieces):
            core_copy(i, j).wait_send()
            if i < chips - 1:
                chip_copy(i, j).wait_send()


def solution(mesh):
    seq_count, tensor_count = mesh.shape["seq"], mesh.shape["tensor"]

    def body(queries, keys, values, out_weight, doc_lengths, stretch_place):
        rows, q_width = queries.shape
        kv_width = keys.shape[1]
        model = out_weight.shape[1]
        kv_local = kv_width // HD
        wide = q_width // kv_width * rows
        chips = tensor_count // 2
        chunk = model // tensor_count
        pieces = max(1, chunk // 512)
        width = chunk // pieces
        smem = pl.BlockSpec(memory_space=pltpu.SMEM)
        anywhere = pl.BlockSpec(memory_space=pltpu.HBM)
        dma = pltpu.SemaphoreType.DMA
        total = pl.pallas_call(
            functools.partial(kernel, seq_count, tensor_count, pieces),
            out_shape=jax.ShapeDtypeStruct((rows, chunk), F32),
            in_specs=[smem, smem] + [anywhere] * 4,
            out_specs=pl.BlockSpec(memory_space=pltpu.VMEM),
            scratch_shapes=[
                pltpu.VMEM((rows, q_width), BF16),
                pltpu.VMEM((rows, kv_width), BF16),
                pltpu.VMEM((seq_count, rows, kv_width), BF16),
                pltpu.VMEM((seq_count, rows, kv_width), BF16),
                pltpu.VMEM((kv_local, wide, HD), BF16),
                pltpu.VMEM((tensor_count, q_width, chunk), BF16),
                pltpu.VMEM((rows, q_width), BF16),
                pltpu.VMEM((kv_local, 1, wide), F32),
                pltpu.VMEM((kv_local, 1, wide), F32),
                pltpu.VMEM((kv_local, HD, wide), F32),
                pltpu.VMEM((chips, pieces, rows, width), F32),
                pltpu.VMEM((chips, pieces, rows, width), BF16),
                pltpu.VMEM((chips, pieces, rows, width), BF16),
                pltpu.VMEM((chips - 1, pieces, rows, width), BF16),
                pltpu.VMEM((chips - 1, pieces, rows, width), BF16),
                dma((3 + tensor_count,)),
                dma((2 + max(1, min(seq_count // 2, DIRECT_MOST) - 1), seq_count // 2, 2)),
                dma((seq_count, 2)),
                dma((chips, pieces)),
                dma((chips, pieces)),
                dma((chips - 1, pieces)),
                dma((chips - 1, pieces)),
            ],
            compiler_params=pltpu.CompilerParams(
                collective_id=0, has_side_effects=True, vmem_limit_bytes=VMEM_LIMIT
            ),
            name="attention_layer",
        )(*[
            pltpu.with_memory_space_constraint(x, pltpu.HBM)
            for x in (doc_lengths, stretch_place, queries, keys, values, out_weight)
        ])
        return total.astype(BF16)

    in_specs = (
        P("seq", "tensor"),
        P("seq", "tensor"),
        P("seq", "tensor"),
        P("tensor", None),
        P(),
        P(),
    )
    return jax.shard_map(
        body, mesh=mesh, in_specs=in_specs, out_specs=P("seq", "tensor"), check_vma=False
    )
```

```python
import functools
import math

import jax
import jax.numpy as jnp
from jax import lax
from jax.experimental import pallas as pl
from jax.experimental.pallas import tpu as pltpu
from jax.sharding import PartitionSpec as P

HD = 128
ROPE_BASE = 500000.0
MASKED = -1e30
FLOOR = -5e29
F32 = jnp.float32
BF16 = jnp.bfloat16
MESH = pl.DeviceIdType.MESH
UNROLL_MOST = 8
DIRECT_MOST = 2
VMEM_LIMIT = 50 * 1024 * 1024


def kernel(
    seq_count,
    tensor_count,
    pieces,
    lengths_ref,
    place_ref,
    q_hbm,
    k_hbm,
    v_hbm,
    w_hbm,
    out_ref,
    q_in,
    k_in,
    gk,
    gv,
    qs,
    w_buf,
    attended,
    run_max,
    run_total,
    accum,
    kept,
    send_core,
    recv_core,
    send_chip,
    recv_chip,
    load_sem,
    gather_send,
    gather_recv,
    core_send_sem,
    core_recv_sem,
    chip_send_sem,
    chip_recv_sem,
):
    rows = q_in.shape[0]
    half_rows = rows // 2
    kv_local = k_in.shape[1] // HD
    group = q_in.shape[1] // k_in.shape[1]
    wide = group * rows
    line = seq_count // 2
    chips = tensor_count // 2
    chunk = w_buf.shape[2]
    width = chunk // pieces

    me = lax.axis_index("seq")
    p, y = me // 2, me % 2
    t = lax.axis_index("tensor")
    a, c = t // 2, t % 2
    has_up, has_down = p < line - 1, p > 0
    direct = 2 < line <= DIRECT_MOST
    from_end = lambda place: (place == 0) | (place == line - 1)
    beside = p * 2 + (1 - y)
    other_core = a * 2 + (1 - c)

    loads = [
        pltpu.make_async_copy(k_hbm, k_in, load_sem.at[0]),
        pltpu.make_async_copy(v_hbm, gv.at[me], load_sem.at[1]),
        pltpu.make_async_copy(q_hbm, q_in, load_sem.at[2]),
    ]
    for load in loads:
        load.start()

    barrier = pltpu.get_barrier_semaphore()

    def greet(where):
        pl.semaphore_signal(barrier, inc=1, device_id=where, device_id_type=MESH)

    greet({"seq": beside})
    greet({"tensor": other_core})
    for i in range(1, chips):
        greet({"tensor": (a + i) % chips * 2 + c})

    @pl.when(has_up)
    def _():
        greet({"seq": me + 2})

    @pl.when(has_down)
    def _():
        greet({"seq": me - 2})

    base0 = place_ref[2 * me] * half_rows
    base1 = place_ref[2 * me + 1] * half_rows

    def positions(shape, axis):
        row = lax.broadcasted_iota(jnp.int32, shape, axis) % rows
        return jnp.where(row < half_rows, base0 + row, base1 + row - half_rows)

    lane = lax.broadcasted_iota(jnp.int32, (rows, HD), 1)
    freq = jnp.exp((lane % (HD // 2)).astype(F32) * (-2.0 / HD * math.log(ROPE_BASE)))
    angle = positions((rows, HD), 0).astype(F32) * freq
    cosine = jnp.cos(angle)
    sine = jnp.where(lane < HD // 2, -jnp.sin(angle), jnp.sin(angle))

    greeted = 1 + chips + has_up.astype(jnp.int32) + has_down.astype(jnp.int32)
    if direct:
        for apart in range(2, line):

            @pl.when(p + apart < line)
            def _():
                @pl.when((p == 0) | (p + apart == line - 1))
                def _():
                    greet({"seq": me + 2 * apart})

            @pl.when(p - apart >= 0)
            def _():
                @pl.when((p == line - 1) | (p - apart == 0))
                def _():
                    greet({"seq": me - 2 * apart})

            above = (p + apart < line) & ((p == 0) | (p + apart == line - 1))
            below = (p - apart >= 0) & ((p == line - 1) | (p - apart == 0))
            greeted = greeted + above.astype(jnp.int32) + below.astype(jnp.int32)
    pl.semaphore_wait(barrier, greeted)

    def far_target(apart):
        return me + jnp.where(p == 0, 2 * apart, -2 * apart)

    def gather_copy(way, block, kind, own=False):
        buf = gk if kind == 0 else gv
        src = v_hbm if own and kind == 1 else buf.at[block]
        target = (me + 2, me - 2, beside)[way] if way < 3 else far_target(way - 1)
        return pltpu.make_async_remote_copy(
            src_ref=src,
            dst_ref=buf.at[block],
            send_sem=gather_send.at[way, block // 2, kind],
            recv_sem=gather_recv.at[block, kind],
            device_id={"seq": target},
            device_id_type=MESH,
        )

    def send_own(kind):
        if direct:
            for apart in range(line - 1, 1, -1):

                @pl.when(from_end(p))
                def _():
                    gather_copy(apart + 1, me, kind, True).start()

        @pl.when(has_up)
        def _():
            gather_copy(0, me, kind, True).start()

        @pl.when(has_down)
        def _():
            gather_copy(1, me, kind, True).start()

        gather_copy(2, me, kind, True).start()

    def arrived(block, kind):
        gather_copy(2, block, kind).wait_recv()

    def forward(place, kind):
        block = place * 2 + y

        keep = from_end(place) if direct else place != place

        @pl.when((place < p) & has_up & ~keep)
        def _():
            gather_copy(0, block, kind).start()

        @pl.when((place > p) & has_down & ~keep)
        def _():
            gather_copy(1, block, kind).start()

        gather_copy(2, block, kind).start()

    send_own(1)

    def owner(slot):
        i = slot // 2 + 1
        return (a + i) % chips * 2 + jnp.where(slot % 2 == 0, 1 - c, c)

    weight_loads = []
    for slot in range(tensor_count):
        start = pl.multiple_of(owner(slot) * chunk, 128)
        weight_loads.append(
            pltpu.make_async_copy(
                w_hbm.at[:, pl.ds(start, chunk)], w_buf.at[slot], load_sem.at[3 + slot]
            )
        )

    def rotate(block):
        floats = block.astype(F32)
        return (floats * cosine + pltpu.roll(floats, HD // 2, 1) * sine).astype(BF16)

    loads[0].wait()
    for h in range(kv_local):
        gk[me, :, h * HD : (h + 1) * HD] = rotate(k_in[:, h * HD : (h + 1) * HD])
    send_own(0)
    for load in weight_loads:
        load.start()

    near = jnp.minimum(p, line - 1 - p)

    def nth_place(k):
        apart = (k + 1) // 2
        both = jnp.where(k % 2 == 1, p - apart, p + apart)
        single = jnp.where(p < line - 1 - p, p + (k - near), p - (k - near))
        return jnp.where(k <= 2 * near, both, single)

    def relay(k):
        place = nth_place(k)
        for kind in (1, 0):
            arrived(place * 2 + y, kind)
            forward(place, kind)

    for k in range(1, min(3, line)):
        relay(jnp.int32(k))

    loads[2].wait()
    for h in range(kv_local):
        for g in range(group):
            column = (h * group + g) * HD
            qs[h, g * rows : (g + 1) * rows, :] = rotate(q_in[:, column : column + HD])

    last = positions((1, wide), 1)
    first = jnp.zeros((1, wide), jnp.int32)
    end = jnp.int32(0)
    for i in range(lengths_ref.shape[0]):
        end = end + lengths_ref[i]
        first = jnp.maximum(first, jnp.where(end <= last, end, 0))

    run_max[...] = jnp.full_like(run_max, FLOOR)
    run_total[...] = jnp.zeros_like(run_total)
    accum[...] = jnp.zeros_like(accum)
    scale = math.log2(math.e) / math.sqrt(HD)

    def attend(block):
        row = lax.broadcasted_iota(jnp.int32, (half_rows, wide), 0)
        allowed = []
        for j in range(2):
            base = place_ref[2 * block + j] * half_rows
            allowed.append((row >= first - base) & (row <= last - base))
        for h in range(kv_local):
            key = gk[block, :, h * HD : (h + 1) * HD]
            value = gv[block, :, h * HD : (h + 1) * HD]
            scores = lax.dot_general(
                key, qs[h], (((1,), (1,)), ((), ())), preferred_element_type=F32
            )
            scores = jnp.concatenate(
                [
                    jnp.where(allowed[j], scores[j * half_rows : (j + 1) * half_rows], MASKED)
                    for j in range(2)
                ],
                axis=0,
            )
            old = run_max[h]
            new = jnp.maximum(old, jnp.max(scores, axis=0, keepdims=True))
            weights = jnp.exp2((scores - new) * scale)
            factor = jnp.exp2((old - new) * scale)
            run_max[h] = new
            run_total[h] = run_total[h] * factor + jnp.sum(weights, axis=0, keepdims=True)
            accum[h] = accum[h] * factor + lax.dot_general(
                value,
                weights.astype(BF16),
                (((0,), (0,)), ((), ())),
                preferred_element_type=F32,
            )

    loads[1].wait()
    attend(me)

    def attend_across(k):
        across = nth_place(k) * 2 + (1 - y)
        for kind in (1, 0):
            arrived(across, kind)
        attend(across)

    def step(k):
        attend(nth_place(k) * 2 + y)

        @pl.when(k + 2 < line)
        def _():
            relay(k + 2)

        @pl.when(k > 1)
        def _():
            attend_across(k - 2)

    def repeat(low, high, body):
        if high - low < UNROLL_MOST:
            for k in range(low, high):
                body(jnp.int32(k))
        else:

            def one(k, carry):
                body(k)
                return carry

            lax.fori_loop(low, high, one, 0)

    repeat(1, line, step)
    for k in range(max(0, line - 2), line):
        attend_across(jnp.int32(k))

    for h in range(kv_local):
        mixed = (accum[h] * (1.0 / run_total[h])).T.astype(BF16)
        for g in range(group):
            column = (h * group + g) * HD
            attended[:, column : column + HD] = mixed[g * rows : (g + 1) * rows]

    def partial_sum(slot, j):
        return jnp.dot(
            attended[...],
            w_buf[slot, :, j * width : (j + 1) * width],
            preferred_element_type=F32,
        )

    def core_copy(i, j):
        return pltpu.make_async_remote_copy(
            src_ref=send_core.at[i, j],
            dst_ref=recv_core.at[i, j],
            send_sem=core_send_sem.at[i, j],
            recv_sem=core_recv_sem.at[i, j],
            device_id={"tensor": other_core},
            device_id_type=MESH,
        )

    def chip_copy(i, j):
        return pltpu.make_async_remote_copy(
            src_ref=send_chip.at[i, j],
            dst_ref=recv_chip.at[i, j],
            send_sem=chip_send_sem.at[i, j],
            recv_sem=chip_recv_sem.at[i, j],
            device_id={"tensor": (a + i + 1) % chips * 2 + c},
            device_id_type=MESH,
        )

    def pass_on(i, j):
        core_copy(i, j).wait_recv()
        send_chip[i, j] = (kept[i, j] + recv_core[i, j].astype(F32)).astype(BF16)
        chip_copy(i, j).start()

    waiting = []
    for i in range(chips):
        for j in range(pieces):
            if j == 0:
                weight_loads[2 * i].wait()
            send_core[i, j] = partial_sum(2 * i, j).astype(BF16)
            core_copy(i, j).start()
            if j == 0:
                weight_loads[2 * i + 1].wait()
            kept[i, j] = partial_sum(2 * i + 1, j)
            if waiting:
                pass_on(*waiting.pop())
            if i < chips - 1:
                waiting.append((i, j))
    for j in range(pieces):
        core_copy(chips - 1, j).wait_recv()
        total = kept[chips - 1, j] + recv_core[chips - 1, j].astype(F32)
        for i in range(chips - 1):
            chip_copy(i, j).wait_recv()
            total = total + recv_chip[i, j].astype(F32)
        out_ref[:, j * width : (j + 1) * width] = total

    def drain(place):
        block = place * 2 + y
        keep = from_end(place) & (place != p) if direct else place != place
        for kind in (1, 0):

            @pl.when((place <= p) & has_up & ~keep)
            def _():
                gather_copy(0, block, kind).wait_send()

            @pl.when((place >= p) & has_down & ~keep)
            def _():
                gather_copy(1, block, kind).wait_send()

            gather_copy(2, block, kind).wait_send()

    repeat(0, line, drain)
    if direct:
        for apart in range(line - 1, 1, -1):
            for kind in (1, 0):

                @pl.when(from_end(p))
                def _():
                    gather_copy(apart + 1, me, kind).wait_send()

    for i in range(chips):
        for j in range(pieces):
            core_copy(i, j).wait_send()
            if i < chips - 1:
                chip_copy(i, j).wait_send()


def solution(mesh):
    seq_count, tensor_count = mesh.shape["seq"], mesh.shape["tensor"]

    def body(queries, keys, values, out_weight, doc_lengths, stretch_place):
        rows, q_width = queries.shape
        kv_width = keys.shape[1]
        model = out_weight.shape[1]
        kv_local = kv_width // HD
        wide = q_width // kv_width * rows
        chips = tensor_count // 2
        chunk = model // tensor_count
        pieces = max(1, chunk // 512)
        width = chunk // pieces
        smem = pl.BlockSpec(memory_space=pltpu.SMEM)
        anywhere = pl.BlockSpec(memory_space=pltpu.HBM)
        dma = pltpu.SemaphoreType.DMA
        total = pl.pallas_call(
            functools.partial(kernel, seq_count, tensor_count, pieces),
            out_shape=jax.ShapeDtypeStruct((rows, chunk), F32),
            in_specs=[smem, smem] + [anywhere] * 4,
            out_specs=pl.BlockSpec(memory_space=pltpu.VMEM),
            scratch_shapes=[
                pltpu.VMEM((rows, q_width), BF16),
                pltpu.VMEM((rows, kv_width), BF16),
                pltpu.VMEM((seq_count, rows, kv_width), BF16),
                pltpu.VMEM((seq_count, rows, kv_width), BF16),
                pltpu.VMEM((kv_local, wide, HD), BF16),
                pltpu.VMEM((tensor_count, q_width, chunk), BF16),
                pltpu.VMEM((rows, q_width), BF16),
                pltpu.VMEM((kv_local, 1, wide), F32),
                pltpu.VMEM((kv_local, 1, wide), F32),
                pltpu.VMEM((kv_local, HD, wide), F32),
                pltpu.VMEM((chips, pieces, rows, width), F32),
                pltpu.VMEM((chips, pieces, rows, width), BF16),
                pltpu.VMEM((chips, pieces, rows, width), BF16),
                pltpu.VMEM((chips - 1, pieces, rows, width), BF16),
                pltpu.VMEM((chips - 1, pieces, rows, width), BF16),
                dma((3 + tensor_count,)),
                dma((2 + max(1, min(seq_count // 2, DIRECT_MOST) - 1), seq_count // 2, 2)),
                dma((seq_count, 2)),
                dma((chips, pieces)),
                dma((chips, pieces)),
                dma((chips - 1, pieces)),
                dma((chips - 1, pieces)),
            ],
            compiler_params=pltpu.CompilerParams(
                collective_id=0, has_side_effects=True, vmem_limit_bytes=VMEM_LIMIT
            ),
            name="attention_layer",
        )(*[
            pltpu.with_memory_space_constraint(x, pltpu.HBM)
            for x in (doc_lengths, stretch_place, queries, keys, values, out_weight)
        ])
        return total.astype(BF16)

    in_specs = (
        P("seq", "tensor"),
        P("seq", "tensor"),
        P("seq", "tensor"),
        P("tensor", None),
        P(),
        P(),
    )
    return jax.shard_map(
        body, mesh=mesh, in_specs=in_specs, out_specs=P("seq", "tensor"), check_vma=False
    )
```
